32 devices in a mesh: node: 16 (over z, y, core), local: 2 (over x).
Axes of the slice: x: 2, y: 2, z: 4, core: 2. Of those that a mesh axis runs over, the one named last changes fastest.
Arguments:
- activations: bfloat16 [4096, 4096], P(('node', 'local')), may hold values from -6 to 6
- out_grads: bfloat16 [4096, 512], P(('node', 'local')), may hold values from -6 to 6
- master: float32 [4096, 512], P(('node', 'local')), may hold values from -0.15 to 0.15
- first_moment: float32 [4096, 512], P(('node', 'local')), may hold values from -0.6 to 0.6
- second_moment: float32 [4096, 512], P(('node', 'local')), may hold values from 0.01 to 1
Outputs:
- new_weight: bfloat16 [4096, 512], P('node')
- new_first: float32 [4096, 512], P(('node', 'local'))
- new_second: float32 [4096, 512], P(('node', 'local'))
The draws below stay inside these ranges and needn't reach their ends.
All inputs are finite; a program needn't handle non-finite values.
Results may differ from the reference program's by a relative error of at most 0.009.
Values may be sent and summed in bfloat16 or wider, within the bound.
No kernel may reach another device: no remote copies, remote signals or barrier semaphores. Data moves between devices by JAX's collectives and lax.ppermute only.
A program may use at most 128 MiB of HBM per device.

```python
import math
import jax
import jax.numpy as jnp
from jax import lax

D = 4096
BLOCK = 256
TOK_DEV = 128
KV = 512
TOKENS = 4096
N_NODE = 16
N_LOCAL = 2


def spiked(drawn, stream_key, source, target, parts, factor):
    owner, partner = [(jnp.arange(drawn.shape[dim]) // (drawn.shape[dim] // parts)).reshape([-1 if axis == dim else 1 for axis in range(drawn.ndim)]) for dim in (source, target)]
    chosen = jax.random.permutation(stream_key, parts)[partner]
    strong = (owner == chosen) | (owner == (partner + parts // 2) % parts)
    return jnp.where(strong, factor * drawn, drawn)


def block_scale(rng, dims, split, least, high):
    level, own = 1.0, jax.random.fold_in(rng, 6)
    for position, blocks in split:
        heights = jnp.exp(jax.random.uniform(jax.random.fold_in(own, position), (blocks,), jnp.float32, least / len(split), high / len(split)))
        level = level * jnp.repeat(heights, dims[position] // blocks).reshape([-1 if axis == position else 1 for axis in range(len(dims))])
    return level


def centred(own_key, shape, width, most, pieces=(), held_as=jnp.bfloat16):
    entries = jax.random.normal(own_key, shape, jnp.float32) * width
    if len(pieces) > 0:
        entries = block_scale(own_key, shape, pieces, -0.22, 0.18) * entries
    return jnp.clip(entries, min=-most, max=most).astype(held_as)


def heavy_noise(own_key, extent, spread, reach, shards, heavy, kind=jnp.bfloat16):
    drawn = spread * jax.random.normal(own_key, extent, jnp.float32)
    if shards:
        drawn = drawn * block_scale(own_key, extent, shards, -0.22, 0.18)
    return jnp.clip(spiked(drawn, jax.random.fold_in(own_key, 3), *heavy), -reach, reach).astype(kind)


def setup_inputs(seed: int = 0) -> dict:
    streams_of = jax.random.split(jax.random.key(seed), 6)
    return {
        "activations": heavy_noise(streams_of[0], (TOKENS, D), 1.0, 6.0, ((0, 32),), (0, 1, 32, 2.75)),
        "out_grads": centred(streams_of[1], (TOKENS, KV), 1.0, 6.0, ((0, 32),)),
        "master": centred(streams_of[2], (D, KV), 0.02, 0.15, ((0, 32),), jnp.float32),
        "first_moment": centred(streams_of[3], (D, KV), 0.1, 0.6, ((0, 32),), jnp.float32),
        "second_moment": jnp.clip(jnp.exp(math.log(1.0) - 4.6051702 * jax.random.uniform(streams_of[4], (D, KV), jnp.float32) ** block_scale(streams_of[4], (D, KV), ((0, 32),), -0.2, 0.2)), 0.01, 1.0),
    }


def quantize(values):
    blocks = values.reshape(values.shape[:-1] + (KV // BLOCK, BLOCK))
    largest = lax.optimization_barrier(jnp.max(jnp.abs(blocks), axis=-1, keepdims=True))
    scale = (largest + 1e-06) / 127.0
    payload = (blocks / scale).astype(jnp.bfloat16)
    return (payload, scale)

def restore(payload, scale):
    payload = lax.optimization_barrier(payload)
    values = payload.astype(jnp.float32) * scale
    return values.reshape(values.shape[:-2] + (KV,))

def reference(activations, out_grads, master, first_moment, second_moment):

    def node_step(total, node):

        def local_step(summed, local):
            device = node * N_LOCAL + local
            inputs = lax.dynamic_slice_in_dim(activations, device * TOK_DEV, TOK_DEV, 0)
            outputs = lax.dynamic_slice_in_dim(out_grads, device * TOK_DEV, TOK_DEV, 0)
            grad = jnp.dot(inputs.T, outputs, preferred_element_type=jnp.float32)
            return (summed + restore(*quantize(grad)), None)
        first_sum, unused = lax.scan(local_step, jnp.zeros((D, KV), jnp.float32), jnp.arange(N_LOCAL, dtype=jnp.int32))
        return (total + restore(*quantize(first_sum)), None)
    total, unused = lax.scan(node_step, jnp.zeros((D, KV), jnp.float32), jnp.arange(N_NODE, dtype=jnp.int32))
    grad = total / (N_NODE * N_LOCAL)
    new_first = 0.9 * first_moment + 0.1 * grad
    new_second = 0.95 * second_moment + 0.05 * grad * grad
    update = new_first / (1.0 - 0.9 ** 10) / (jnp.sqrt(new_second / (1.0 - 0.95 ** 10)) + 1e-08)
    new_weight = (master - 0.01 * update).astype(jnp.bfloat16)
    return (new_weight, new_first, new_second)
```

```python
import functools

import jax
import jax.numpy as jnp
from jax import lax
from jax.experimental import pallas as pl
from jax.experimental.pallas import tpu as pltpu
from jax.sharding import PartitionSpec as P


def partner(index, step, count):
    if count & (count - 1) == 0:
        return index ^ step
    return (index + step) % count


class Layout:
    def __init__(self, node_count, local_count):
        self.core = 2 if node_count % 2 == 0 else 1
        rest = node_count // self.core
        self.middle = 2 if rest % 2 == 0 else 1
        self.outer = rest // self.middle
        self.local = local_count
        self.group = self.middle * self.local

    def split(self, device):
        node, local = device // self.local, device % self.local
        core, rest = node % self.core, node // self.core
        return rest // self.middle, rest % self.middle, core, local

    def join(self, outer, middle, core, local):
        return ((outer * self.middle + middle) * self.core + core) * self.local + local

    def move(self, device, outer=0, group=0, core=0):
        o, m, c, l = self.split(device)
        return self.join(
            partner(o, outer, self.outer),
            partner(m, group // self.local, self.middle),
            partner(c, core, self.core),
            partner(l, group % self.local, self.local),
        )

    def permute(self, value, **steps):
        count = self.outer * self.middle * self.core * self.local
        pairs = [(d, self.move(d, **steps)) for d in range(count)]
        return lax.ppermute(value, ("node", "local"), pairs)

    def me(self):
        return lax.axis_index("node") * self.local + lax.axis_index("local")


def in_vmem(value):
    return pltpu.with_memory_space_constraint(value, pltpu.VMEM)


def take_kernel(grid, wanted, rows, source, *outs):
    me = grid.me()
    for (group, steps), out in zip(wanted, outs):
        for j, (o, c) in enumerate((o, c) for c in range(grid.core) for o in steps):
            block = grid.move(me, outer=o, group=group, core=c)
            columns = pl.ds(pl.multiple_of(block * rows, rows), rows)
            out[:, pl.ds(j * rows, rows)] = source[:, columns]


def take(grid, wanted, rows, activations):
    tokens = activations.shape[0]
    if rows % 128:
        me = grid.me()
        out = []
        for group, steps in wanted:
            blocks = [
                grid.move(me, outer=o, group=group, core=c) for c in range(grid.core) for o in steps
            ]
            parts = [lax.dynamic_slice_in_dim(activations, b * rows, rows, 1) for b in blocks]
            out.append(jnp.concatenate(parts, 1))
        return out
    vmem = pl.BlockSpec(memory_space=pltpu.VMEM)
    return pl.pallas_call(
        functools.partial(take_kernel, grid, wanted, rows),
        out_shape=[
            pltpu.VMEM((tokens, len(steps) * grid.core * rows), activations.dtype)
            for _, steps in wanted
        ],
        in_specs=[vmem],
        out_specs=[vmem] * len(wanted),
        name="take",
    )(activations)


def product(left, right):
    return lax.dot_general(
        left, right, (((0,), (0,)), ((), ())), preferred_element_type=jnp.float32
    )


def sums_kernel(members, core_count, *refs):
    lefts, rights = refs[:members], refs[members : 2 * members]
    kept, sent = refs[2 * members :]
    size = kept.shape[0]
    for c in range(core_count):
        at = pl.ds(c * size, size)
        total = None
        for left, right in zip(lefts, rights):
            part = product(left[:, at], right[...])
            total = part if total is None else total + part
        if c == 0:
            kept[...] = total
        else:
            sent[c - 1] = total.astype(sent.dtype)


def group_sums(grid, rows, lefts, rights):
    size = lefts[0].shape[1] // grid.core
    cols = rights[0].shape[1]
    if rows % 128:
        total = product(jnp.concatenate(lefts, 0), jnp.concatenate(rights, 0))
        total = total.reshape(grid.core, size, cols)
        return total[0], total[1:].astype(jnp.bfloat16)
    vmem = pl.BlockSpec(memory_space=pltpu.VMEM)
    members = len(lefts)
    return pl.pallas_call(
        functools.partial(sums_kernel, members, grid.core),
        out_shape=(
            pltpu.VMEM((size, cols), jnp.float32),
            pltpu.VMEM((max(grid.core - 1, 1), size, cols), jnp.bfloat16),
        ),
        in_specs=[vmem] * (2 * members),
        out_specs=(vmem, vmem),
        name="sums",
    )(*(in_vmem(v) for v in (*lefts, *rights)))


def per_device(activations, out_grads, master, first_moment, second_moment):
    grid = Layout(lax.axis_size("node"), lax.axis_size("local"))
    rows = master.shape[0]
    device_count = grid.outer * grid.middle * grid.core * grid.local
    groups = range(1, grid.group)
    half = grid.outer // 2
    far, near = tuple(range(half, grid.outer)), tuple(range(half))

    rights = [out_grads] + [grid.permute(out_grads, group=g) for g in groups]
    far_messages = take(grid, [(g, far) for g in groups], rows, activations)
    far_lefts = [grid.permute(m, group=g) for g, m in zip(groups, far_messages)]
    rest = [(g, near) for g in groups] + [(0, far), (0, near)]
    *near_messages, far_own, near_own = take(grid, rest, rows, activations)
    near_lefts = [grid.permute(m, group=g) for g, m in zip(groups, near_messages)]

    def summed(lefts, count):
        kept, sent = group_sums(grid, rows, lefts, rights)
        for c in range(1, grid.core):
            kept = kept + grid.permute(sent[c - 1], core=c).astype(jnp.float32)
        return [kept[i * rows : (i + 1) * rows] for i in range(count)]

    def send(step, part):
        return grid.permute(part.astype(jnp.bfloat16), outer=step).astype(jnp.float32)

    far_parts = summed([far_own] + far_lefts, len(far))
    near_lefts, far_parts = lax.optimization_barrier((near_lefts, far_parts))
    received = [send(step, part) for step, part in zip(far, far_parts)]
    near_parts = summed([near_own] + near_lefts, len(near))
    received += [send(step, part) for step, part in zip(near[1:], near_parts[1:])]
    total = near_parts[0] + sum(received)

    grad_mean = total / device_count
    new_first = 0.9 * first_moment + 0.1 * grad_mean
    new_second = 0.95 * second_moment + 0.05 * grad_mean * grad_mean
    update = new_first / (1.0 - 0.9**10) / (jnp.sqrt(new_second / (1.0 - 0.95**10)) + 1e-08)
    own_weight = (master - 0.01 * update).astype(jnp.bfloat16)
    new_weight = lax.all_gather(own_weight, "local", axis=0, tiled=True)
    return (new_weight, new_first, new_second)


def solution(mesh):
    spec = P(("node", "local"), None)
    return jax.shard_map(
        per_device,
        mesh=mesh,
        in_specs=(spec,) * 5,
        out_specs=(P("node", None), spec, spec),
        check_vma=False,
    )
```

```python
import functools

import jax
import jax.numpy as jnp
from jax import lax
from jax.experimental import pallas as pl
from jax.experimental.pallas import tpu as pltpu
from jax.sharding import PartitionSpec as P


def partner(index, step, count):
    if count & (count - 1) == 0:
        return index ^ step
    return (index + step) % count


class Layout:
    def __init__(self, node_count, local_count):
        self.core = 2 if node_count % 2 == 0 else 1
        rest = node_count // self.core
        self.middle = 2 if rest % 2 == 0 else 1
        self.outer = rest // self.middle
        self.local = local_count
        self.group = self.middle * self.local

    def split(self, device):
        node, local = device // self.local, device % self.local
        core, rest = node % self.core, node // self.core
        return rest // self.middle, rest % self.middle, core, local

    def join(self, outer, middle, core, local):
        return ((outer * self.middle + middle) * self.core + core) * self.local + local

    def move(self, device, outer=0, group=0, core=0):
        o, m, c, l = self.split(device)
        return self.join(
            partner(o, outer, self.outer),
            partner(m, group // self.local, self.middle),
            partner(c, core, self.core),
            partner(l, group % self.local, self.local),
        )

    def permute(self, value, **steps):
        count = self.outer * self.middle * self.core * self.local
        pairs = [(d, self.move(d, **steps)) for d in range(count)]
        return lax.ppermute(value, ("node", "local"), pairs)

    def me(self):
        return lax.axis_index("node") * self.local + lax.axis_index("local")


def in_vmem(value):
    return pltpu.with_memory_space_constraint(value, pltpu.VMEM)


def take_kernel(grid, wanted, rows, source, *outs):
    me = grid.me()
    for (group, steps), out in zip(wanted, outs):
        for j, (o, c) in enumerate((o, c) for c in range(grid.core) for o in steps):
            block = grid.move(me, outer=o, group=group, core=c)
            columns = pl.ds(pl.multiple_of(block * rows, rows), rows)
            out[:, pl.ds(j * rows, rows)] = source[:, columns]


def take(grid, wanted, rows, activations):
    tokens = activations.shape[0]
    if rows % 128:
        me = grid.me()
        out = []
        for group, steps in wanted:
            blocks = [
                grid.move(me, outer=o, group=group, core=c) for c in range(grid.core) for o in steps
            ]
            parts = [lax.dynamic_slice_in_dim(activations, b * rows, rows, 1) for b in blocks]
            out.append(jnp.concatenate(parts, 1))
        return out
    vmem = pl.BlockSpec(memory_space=pltpu.VMEM)
    return pl.pallas_call(
        functools.partial(take_kernel, grid, wanted, rows),
        out_shape=[
            pltpu.VMEM((tokens, len(steps) * grid.core * rows), activations.dtype)
            for _, steps in wanted
        ],
        in_specs=[vmem],
        out_specs=[vmem] * len(wanted),
        name="take",
    )(activations)


def product(left, right):
    return lax.dot_general(
        left, right, (((0,), (0,)), ((), ())), preferred_element_type=jnp.float32
    )


def sums_kernel(members, core_count, *refs):
    lefts, rights = refs[:members], refs[members : 2 * members]
    kept, sent = refs[2 * members :]
    size = kept.shape[0]
    for c in range(core_count):
        at = pl.ds(c * size, size)
        total = None
        for left, right in zip(lefts, rights):
            part = product(left[:, at], right[...])
            total = part if total is None else total + part
        if c == 0:
            kept[...] = total
        else:
            sent[c - 1] = total.astype(sent.dtype)


def group_sums(grid, rows, lefts, rights):
    size = lefts[0].shape[1] // grid.core
    cols = rights[0].shape[1]
    if rows % 128:
        total = product(jnp.concatenate(lefts, 0), jnp.concatenate(rights, 0))
        total = total.reshape(grid.core, size, cols)
        return total[0], total[1:].astype(jnp.bfloat16)
    vmem = pl.BlockSpec(memory_space=pltpu.VMEM)
    members = len(lefts)
    return pl.pallas_call(
        functools.partial(sums_kernel, members, grid.core),
        out_shape=(
            pltpu.VMEM((size, cols), jnp.float32),
            pltpu.VMEM((max(grid.core - 1, 1), size, cols), jnp.bfloat16),
        ),
        in_specs=[vmem] * (2 * members),
        out_specs=(vmem, vmem),
        name="sums",
    )(*(in_vmem(v) for v in (*lefts, *rights)))


def update_kernel(scale, kept, own_core, *refs):
    *hops, master, first_moment, second_moment, weight, new_first, new_second = refs
    rows = master.shape[0]
    total = kept[pl.ds(0, rows), :] + own_core[pl.ds(0, rows), :].astype(jnp.float32)
    for hop in hops:
        total += hop[...].astype(jnp.float32)
    grad = total * scale
    first = 0.9 * first_moment[...] + 0.1 * grad
    second = 0.95 * second_moment[...] + 0.05 * grad * grad
    update = first / (1.0 - 0.9**10) / (jnp.sqrt(second / (1.0 - 0.95**10)) + 1e-08)
    weight[...] = (master[...] - 0.01 * update).astype(weight.dtype)
    new_first[...] = first
    new_second[...] = second


def adam(count, kept, own_core, hops, master, first_moment, second_moment):
    vmem = pl.BlockSpec(memory_space=pltpu.VMEM)
    shape = master.shape
    operands = (kept, own_core, *hops, master, first_moment, second_moment)
    return pl.pallas_call(
        functools.partial(update_kernel, 1.0 / count),
        out_shape=(
            pltpu.VMEM(shape, jnp.bfloat16),
            pltpu.VMEM(shape, jnp.float32),
            pltpu.VMEM(shape, jnp.float32),
        ),
        in_specs=[vmem] * len(operands),
        out_specs=(vmem,) * 3,
        name="adam",
    )(*(in_vmem(v) for v in operands))


def join_kernel(own, other, out, sems):
    rows = own.shape[0]
    mine = lax.axis_index("local")
    copies = [
        pltpu.make_async_copy(part, out.at[pl.ds(at * rows, rows), :], sem)
        for part, at, sem in ((own, mine, sems.at[0]), (other, 1 - mine, sems.at[1]))
    ]
    for copy in copies:
        copy.start()
    for copy in copies:
        copy.wait()


def joined(grid, own):
    if grid.local != 2 or own.shape[0] % 128:
        return lax.all_gather(own, "local", axis=0, tiled=True)
    other = grid.permute(own, group=1)
    vmem = pl.BlockSpec(memory_space=pltpu.VMEM)
    return pl.pallas_call(
        join_kernel,
        out_shape=jax.ShapeDtypeStruct((2 * own.shape[0], own.shape[1]), own.dtype),
        in_specs=[vmem, vmem],
        out_specs=pl.BlockSpec(memory_space=pl.ANY),
        scratch_shapes=[pltpu.SemaphoreType.DMA((2,))],
        name="join",
    )(in_vmem(own), in_vmem(other))


def step(activations, out_grads, master, first_moment, second_moment):
    grid = Layout(lax.axis_size("node"), lax.axis_size("local"))
    rows = master.shape[0]
    count = grid.outer * grid.middle * grid.core * grid.local
    groups = range(1, grid.group)
    half = grid.outer // 2
    far, near = tuple(range(half, grid.outer)), tuple(range(half))

    rights = [out_grads] + [grid.permute(out_grads, group=g) for g in groups]
    messages = take(grid, [(g, far) for g in groups], rows, activations)
    far_lefts = [grid.permute(m, group=g) for g, m in zip(groups, messages)]
    rest = [(g, near) for g in groups] + [(0, far), (0, near)]
    *messages, far_own, near_own = take(grid, rest, rows, activations)
    near_lefts = [grid.permute(m, group=g) for g, m in zip(groups, messages)]

    kept, sent = group_sums(grid, rows, [far_own] + far_lefts, rights)
    got = [grid.permute(sent[c - 1], core=c) for c in range(1, grid.core)]
    parts = sum([g.astype(jnp.float32) for g in got], kept).astype(jnp.bfloat16)
    hops = [
        grid.permute(parts[i * rows : (i + 1) * rows], outer=o) for i, o in enumerate(far)
    ]
    kept, sent = group_sums(grid, rows, [near_own] + near_lefts, rights)
    got = [grid.permute(sent[c - 1], core=c) for c in range(1, grid.core)]
    for i, o in enumerate(near):
        if i:
            at = slice(i * rows, (i + 1) * rows)
            part = sum([g[at].astype(jnp.float32) for g in got], kept[at])
            hops.append(grid.permute(part.astype(jnp.bfloat16), outer=o))
    if rows % 128 or grid.core != 2:
        total = sum([g[:rows].astype(jnp.float32) for g in got + hops], kept[:rows])
        grad_mean = total / count
        new_first = 0.9 * first_moment + 0.1 * grad_mean
        new_second = 0.95 * second_moment + 0.05 * grad_mean * grad_mean
        root = jnp.sqrt(new_second / (1.0 - 0.95**10)) + 1e-08
        update = new_first / (1.0 - 0.9**10) / root
        own_weight = (master - 0.01 * update).astype(jnp.bfloat16)
    else:
        own_weight, new_first, new_second = adam(
            count, kept, got[0], hops, master, first_moment, second_moment
        )
    new_weight = joined(grid, own_weight)
    return (new_weight, new_first, new_second)


def solution(mesh):
    spec = P(("node", "local"), None)
    return jax.shard_map(
        step,
        mesh=mesh,
        in_specs=(spec,) * 5,
        out_specs=(P("node", None), spec, spec),
        check_vma=False,
    )
```

```python
import functools

import jax
import jax.numpy as jnp
from jax import lax
from jax.experimental import pallas as pl
from jax.experimental.pallas import tpu as pltpu
from jax.sharding import PartitionSpec as P


def partner(index, step, count):
    if count & (count - 1) == 0:
        return index ^ step
    return (index + step) % count


class Layout:
    def __init__(self, node_count, local_count):
        self.core = 2 if node_count % 2 == 0 else 1
        rest = node_count // self.core
        self.middle = 2 if rest % 2 == 0 else 1
        self.outer = rest // self.middle
        if self.outer & (self.outer - 1):
            self.middle, self.outer = rest, 1
        self.local = local_count
        self.group = self.middle * self.local

    def split(self, device):
        node, local = device // self.local, device % self.local
        core, rest = node % self.core, node // self.core
        return rest // self.middle, rest % self.middle, core, local

    def join(self, outer, middle, core, local):
        return ((outer * self.middle + middle) * self.core + core) * self.local + local

    def move(self, device, outer=0, group=0, core=0):
        o, m, c, l = self.split(device)
        return self.join(
            partner(o, outer, self.outer),
            partner(m, group // self.local, self.middle),
            partner(c, core, self.core),
            partner(l, group % self.local, self.local),
        )

    def permute(self, value, **steps):
        count = self.outer * self.middle * self.core * self.local
        pairs = [(d, self.move(d, **steps)) for d in range(count)]
        return lax.ppermute(value, ("node", "local"), pairs)

    def peers(self):
        both = [(g // self.local, g % self.local) for g in range(1, self.group)]
        both.sort(key=lambda ml: (ml[0] > 0 and ml[1] > 0, ml[1] > 0))
        return tuple(m * self.local + l for m, l in both)

    def me(self):
        return lax.axis_index("node") * self.local + lax.axis_index("local")


def in_vmem(value):
    return pltpu.with_memory_space_constraint(value, pltpu.VMEM)


SMALL = pltpu.CompilerParams(vmem_limit_bytes=16 * 2**20)


def take_kernel(grid, wanted, rows, activations, *refs):
    *outs, source, sem = refs
    load = pltpu.make_async_copy(activations, source, sem)
    load.start()
    load.wait()
    me = grid.me()
    for (group, steps), out in zip(wanted, outs):
        for j, (o, c) in enumerate((o, c) for c in range(grid.core) for o in steps):
            block = grid.move(me, outer=o, group=group, core=c)
            columns = pl.ds(pl.multiple_of(block * rows, rows), rows)
            out[:, pl.ds(j * rows, rows)] = source[:, columns]


def take(grid, wanted, rows, activations):
    tokens = activations.shape[0]
    if rows % 128:
        me = grid.me()
        out = []
        for group, steps in wanted:
            blocks = [
                grid.move(me, outer=o, group=group, core=c) for c in range(grid.core) for o in steps
            ]
            parts = [lax.dynamic_slice_in_dim(activations, b * rows, rows, 1) for b in blocks]
            out.append(jnp.concatenate(parts, 1))
        return out
    return pl.pallas_call(
        functools.partial(take_kernel, grid, wanted, rows),
        out_shape=[
            pltpu.VMEM((tokens, len(steps) * grid.core * rows), activations.dtype)
            for _, steps in wanted
        ],
        in_specs=[pl.BlockSpec(memory_space=pltpu.HBM)],
        out_specs=[pl.BlockSpec(memory_space=pltpu.VMEM)] * len(wanted),
        scratch_shapes=[
            pltpu.VMEM(activations.shape, activations.dtype),
            pltpu.SemaphoreType.DMA(()),
        ],
        compiler_params=SMALL,
        name="take",
    )(pltpu.with_memory_space_constraint(activations, pltpu.HBM))


def product(left, right):
    return lax.dot_general(
        left, right, (((0,), (0,)), ((), ())), preferred_element_type=jnp.float32
    )


def sums_kernel(members, cores, size, *refs):
    rights, lefts, out = refs[:members], refs[members:-1], refs[-1]
    width = out.shape[-1]
    for j, core in enumerate(cores):
        rows = pl.ds(core * size, size)
        for half in range(2):
            total = None
            for left, right in zip(lefts, rights):
                part = product(left[:, rows], right[:, pl.ds(half * width, width)])
                total = part if total is None else total + part
            out[j, half] = total.astype(out.dtype)


def group_sums(grid, rows, cores, dtype, rights, lefts):
    size, width = lefts[0].shape[1] // grid.core, rights[0].shape[1] // 2
    if rows % 128:
        left = jnp.concatenate(lefts, 0).reshape(-1, grid.core, size)
        right = jnp.concatenate(rights, 0)
        total = [product(left[:, core], right).astype(dtype) for core in cores]
        return jnp.stack([jnp.stack(jnp.split(t, 2, axis=1)) for t in total])
    vmem = pl.BlockSpec(memory_space=pltpu.VMEM)
    operands = (*rights, *lefts)
    return pl.pallas_call(
        functools.partial(sums_kernel, len(rights), cores, size),
        out_shape=pltpu.VMEM((len(cores), 2, size, width), dtype),
        in_specs=[vmem] * len(operands),
        out_specs=vmem,
        compiler_params=SMALL,
        name="sums",
    )(*(in_vmem(v) for v in operands))


def merge_kernel(pieces, kept, *refs):
    got, outs = refs[: -len(pieces)], refs[-len(pieces) :]
    for (start, size, dtype), out in zip(pieces, outs):
        at = pl.ds(start, size)
        for half in range(2):
            total = kept[half, at, :]
            for part in got:
                total += part[half, at, :].astype(jnp.float32)
            out[half] = total.astype(dtype)


def merge(kept, got, pieces):
    _, size, width = kept.shape
    if size % 128:
        total = kept + sum([g.astype(jnp.float32) for g in got])
        return [total[:, start : start + size].astype(dtype) for start, size, dtype in pieces]
    vmem = pl.BlockSpec(memory_space=pltpu.VMEM)
    return pl.pallas_call(
        functools.partial(merge_kernel, pieces),
        out_shape=[pltpu.VMEM((2, size, width), dtype) for _, size, dtype in pieces],
        in_specs=[vmem] * (1 + len(got)),
        out_specs=[vmem] * len(pieces),
        compiler_params=SMALL,
        name="merge",
    )(*(in_vmem(v) for v in (kept, *got)))


def adam(grad, master, first_moment, second_moment):
    new_first = 0.9 * first_moment + 0.1 * grad
    new_second = 0.95 * second_moment + 0.05 * grad * grad
    update = new_first / (1.0 - 0.9**10) / (jnp.sqrt(new_second / (1.0 - 0.95**10)) + 1e-08)
    return (master - 0.01 * update).astype(jnp.bfloat16), new_first, new_second


def update_kernel(count, parts, halves, weights, *refs):
    master, first_moment, second_moment = refs[:3]
    outs = refs[3 + parts * len(halves) :]
    width = master.shape[1] // 2
    for i, half in enumerate(halves):
        total = None
        for part in refs[3 + i * parts : 3 + (i + 1) * parts]:
            part = part[half] if len(part.shape) == 3 else part[...]
            total = part if total is None else total + part.astype(jnp.float32)
        at = pl.ds(half * width, width)
        step = adam(total / count, master[:, at], first_moment[:, at], second_moment[:, at])
        if weights:
            outs[0][...] = step[0]
        else:
            outs[0][:, at] = step[1]
            outs[1][:, at] = step[2]


def update(count, parts, halves, weights, state):
    vmem = pl.BlockSpec(memory_space=pltpu.VMEM)
    rows, cols = state[0].shape
    width = cols // 2
    if rows % 128:
        out = []
        for half, arrived in zip(halves, parts):
            total = sum([(a[half] if a.ndim == 3 else a).astype(jnp.float32) for a in arrived])
            at = slice(half * width, (half + 1) * width)
            out.append(adam(total / count, *(v[:, at] for v in state)))
        if weights:
            return [out[0][0]]
        return [jnp.concatenate([o[i] for o in out], 1) for i in (1, 2)]
    operands = [*state, *(v for part in parts for v in part)]
    if weights:
        out_shape = [pltpu.VMEM((rows, width), jnp.bfloat16)]
    else:
        out_shape = [pltpu.VMEM((rows, cols), jnp.float32)] * 2
    return pl.pallas_call(
        functools.partial(update_kernel, count, len(parts[0]), halves, weights),
        out_shape=out_shape,
        in_specs=[vmem] * len(operands),
        out_specs=[vmem] * len(out_shape),
        compiler_params=SMALL,
        name="adam",
    )(*(in_vmem(v) for v in operands))


def join_kernel(*refs):
    *parts, out, sems = refs
    rows, width = parts[0].shape
    mine = lax.axis_index("local")
    copies = []
    for i, part in enumerate(parts):
        row = (mine if i < 2 else 1 - mine) * rows
        copies.append(
            pltpu.make_async_copy(
                part, out.at[pl.ds(row, rows), pl.ds((i % 2) * width, width)], sems.at[i]
            )
        )
    for copy in copies:
        copy.start()
    for copy in copies:
        copy.wait()


def joined(grid, own):
    rows, width = own[0].shape
    if grid.local != 2 or rows % 128:
        return lax.all_gather(jnp.concatenate(own, 1), "local", axis=0, tiled=True)
    other = []
    for half in own:
        other.append(grid.permute(half, group=1))
    vmem = pl.BlockSpec(memory_space=pltpu.VMEM)
    return pl.pallas_call(
        join_kernel,
        out_shape=jax.ShapeDtypeStruct((2 * rows, 2 * width), own[0].dtype),
        in_specs=[vmem] * 4,
        out_specs=pl.BlockSpec(memory_space=pl.ANY),
        scratch_shapes=[pltpu.SemaphoreType.DMA((4,))],
        compiler_params=SMALL,
        name="join",
    )(*(in_vmem(v) for v in (*own, *other)))


def step(activations, out_grads, *state):
    grid = Layout(lax.axis_size("node"), lax.axis_size("local"))
    rows = state[0].shape[0]
    count = grid.outer * grid.middle * grid.core * grid.local
    groups = grid.peers()
    odd, even = tuple(range(3, grid.outer, 2)), tuple(range(2, grid.outer, 2))
    near = tuple(range(1, min(2, grid.outer)))

    def send(messages):
        out = []
        for g, message in zip(groups, messages):
            out.append(grid.permute(message, group=g))
        return out

    rights = [out_grads] + send([out_grads] * len(groups))
    plan = {"a": odd, "b": even + near, "c": (0,)}
    plan = {name: steps for name, steps in plan.items() if steps}
    peers = (*groups, 0)
    taken = take(grid, [(g, steps) for steps in plan.values() for g in peers], rows, activations)
    lefts = {}
    for j, name in enumerate(plan):
        *messages, own = taken[j * len(peers) : (j + 1) * len(peers)]
        lefts[name] = [own] + send(messages)

    half, full = jnp.bfloat16, jnp.float32

    def sums(name):
        got = []
        if grid.core > 1:
            others = tuple(range(1, grid.core))
            sent = group_sums(grid, rows, others, half, rights, lefts[name])
            got = [grid.permute(sent[c - 1], core=c) for c in others]
        kept = group_sums(grid, rows, (0,), full, rights, lefts[name])[0]
        return kept, got

    def hop(part, outer):
        return grid.permute(part.astype(half), outer=outer)

    split = len(even) * rows
    hops = [[], []]
    if odd:
        (part,) = merge(*sums("a"), [(0, split, half)])
        passed = hop(part, 1)
    if near:
        pieces = [(split, rows, half)] + ([(0, split, full)] if odd else [])
        part, *base = merge(*sums("b"), pieces)
        near_hop = hop(part, 1)
        for h in range(2):
            hops[h].append(near_hop)
    if odd:
        for h in range(2):
            part = base[0][h] + passed[h].astype(full)
            for i, o in enumerate(even):
                hops[h].append(hop(part[i * rows : (i + 1) * rows], o))
    kept, got = sums("c")

    totals = [[kept, *got, *hops[h]] for h in range(2)]
    weights = []
    for h in range(2):
        weights += update(count, totals[h : h + 1], [h], True, state)
    new_first, new_second = update(count, totals, [0, 1], False, state)
    new_weight = joined(grid, weights)
    return (new_weight, new_first, new_second)


def solution(mesh):
    spec = P(("node", "local"), None)
    return jax.shard_map(
        step,
        mesh=mesh,
        in_specs=(spec,) * 5,
        out_specs=(P("node", None), spec, spec),
        check_vma=False,
    )
```

```python
import functools

import jax
import jax.numpy as jnp
from jax import lax
from jax.experimental import pallas as pl
from jax.experimental.pallas import tpu as pltpu
from jax.sharding import PartitionSpec as P


def partner(index, step, count):
    if count & (count - 1) == 0:
        return index ^ step
    return (index + step) % count


class Layout:
    def __init__(self, node_count, local_count):
        self.core = 2 if node_count % 2 == 0 else 1
        rest = node_count // self.core
        self.middle = 2 if rest % 2 == 0 else 1
        self.outer = rest // self.middle
        if self.outer & (self.outer - 1):
            self.middle, self.outer = rest, 1
        self.local = local_count
        self.group = self.middle * self.local

    def split(self, device):
        node, local = device // self.local, device % self.local
        core, rest = node % self.core, node // self.core
        return rest // self.middle, rest % self.middle, core, local

    def join(self, outer, middle, core, local):
        return ((outer * self.middle + middle) * self.core + core) * self.local + local

    def move(self, device, outer=0, group=0, core=0):
        o, m, c, l = self.split(device)
        return self.join(
            partner(o, outer, self.outer),
            partner(m, group // self.local, self.middle),
            partner(c, core, self.core),
            partner(l, group % self.local, self.local),
        )

    def permute(self, value, **steps):
        count = self.outer * self.middle * self.core * self.local
        pairs = [(d, self.move(d, **steps)) for d in range(count)]
        return lax.ppermute(value, ("node", "local"), pairs)

    def peers(self):
        both = [(g // self.local, g % self.local) for g in range(1, self.group)]
        both.sort(key=lambda ml: (ml[0] > 0 and ml[1] > 0, ml[1] > 0))
        return tuple(m * self.local + l for m, l in both)

    def me(self):
        return lax.axis_index("node") * self.local + lax.axis_index("local")


def in_vmem(value):
    return pltpu.with_memory_space_constraint(value, pltpu.VMEM)


CUT = 4
SMALL = pltpu.CompilerParams(vmem_limit_bytes=16 * 2**20)


def take_kernel(grid, wanted, rows, source, *outs):
    me = grid.me()
    for (group, steps), out in zip(wanted, outs):
        for j, (o, c) in enumerate((o, c) for c in range(grid.core) for o in steps):
            block = grid.move(me, outer=o, group=group, core=c)
            columns = pl.ds(pl.multiple_of(block * rows, rows), rows)
            out[:, pl.ds(j * rows, rows)] = source[:, columns]


def take(grid, wanted, rows, activations):
    tokens = activations.shape[0]
    if rows % 128:
        me = grid.me()
        out = []
        for group, steps in wanted:
            blocks = [
                grid.move(me, outer=o, group=group, core=c) for c in range(grid.core) for o in steps
            ]
            parts = [lax.dynamic_slice_in_dim(activations, b * rows, rows, 1) for b in blocks]
            out.append(jnp.concatenate(parts, 1))
        return out
    return pl.pallas_call(
        functools.partial(take_kernel, grid, wanted, rows),
        out_shape=[
            pltpu.VMEM((tokens, len(steps) * grid.core * rows), activations.dtype)
            for _, steps in wanted
        ],
        in_specs=[pl.BlockSpec(memory_space=pltpu.VMEM)],
        out_specs=[pl.BlockSpec(memory_space=pltpu.VMEM)] * len(wanted),
        compiler_params=SMALL,
        name="take",
    )(in_vmem(activations))


def product(left, right):
    return lax.dot_general(
        left, right, (((0,), (0,)), ((), ())), preferred_element_type=jnp.float32
    )


def sums_kernel(members, firsts, *refs):
    rights, lefts, out = refs[:members], refs[members:-1], refs[-1]
    size = out.shape[1]
    for j, first in enumerate(firsts):
        total = None
        for left, right in zip(lefts, rights):
            part = product(left[:, pl.ds(first, size)], right[...])
            total = part if total is None else total + part
        out[j] = total.astype(out.dtype)


def group_sums(firsts, size, dtype, rights, lefts):
    cols = rights[0].shape[1]
    if size % 128:
        left, right = jnp.concatenate(lefts, 0), jnp.concatenate(rights, 0)
        return jnp.stack([product(left[:, f : f + size], right).astype(dtype) for f in firsts])
    vmem = pl.BlockSpec(memory_space=pltpu.VMEM)
    operands = (*rights, *lefts)
    return pl.pallas_call(
        functools.partial(sums_kernel, len(rights), firsts),
        out_shape=pltpu.VMEM((len(firsts), size, cols), dtype),
        in_specs=[vmem] * len(operands),
        out_specs=vmem,
        compiler_params=SMALL,
        name="sums",
    )(*(in_vmem(v) for v in operands))


def adam(grad, master, first_moment, second_moment):
    new_first = 0.9 * first_moment + 0.1 * grad
    new_second = 0.95 * second_moment + 0.05 * grad * grad
    update = new_first / (1.0 - 0.9**10) / (jnp.sqrt(new_second / (1.0 - 0.95**10)) + 1e-08)
    return (master - 0.01 * update).astype(jnp.bfloat16), new_first, new_second


def update_kernel(count, cuts, weights, shared, *refs):
    master, first_moment, second_moment = refs[:3]
    common, refs = refs[3 : 3 + shared], refs[3 + shared :]
    outs = refs[-1:] if weights else refs[-2:]
    own = (len(refs) - len(outs)) // len(cuts)
    for i, (start, width) in enumerate(cuts):
        at = pl.ds(start, width)
        total = common[0][:, at]
        for part in common[1:]:
            total += part[:, at].astype(jnp.float32)
        for part in refs[i * own : (i + 1) * own]:
            total += part[...].astype(jnp.float32)
        step = adam(total / count, master[:, at], first_moment[:, at], second_moment[:, at])
        if weights:
            outs[0][...] = step[0]
        else:
            outs[0][:, at] = step[1]
            outs[1][:, at] = step[2]


def update(count, cuts, weights, state, common, parts):
    rows, cols = state[0].shape
    if rows % 128:
        out = []
        for (start, width), part in zip(cuts, parts):
            at = slice(start, start + width)
            total = sum([v[:, at].astype(jnp.float32) for v in common])
            total = sum([v.astype(jnp.float32) for v in part], total)
            out.append(adam(total / count, *(v[:, at] for v in state)))
        return [jnp.concatenate([o[i] for o in out], 1) for i in ((0,) if weights else (1, 2))]
    vmem = pl.BlockSpec(memory_space=pltpu.VMEM)
    operands = [*state, *common, *(v for part in parts for v in part)]
    if weights:
        out_shape = [pltpu.VMEM((rows, cuts[0][1]), jnp.bfloat16)]
    else:
        out_shape = [pltpu.VMEM((rows, cols), jnp.float32)] * 2
    return pl.pallas_call(
        functools.partial(update_kernel, count, cuts, weights, len(common)),
        out_shape=out_shape,
        in_specs=[vmem] * len(operands),
        out_specs=[vmem] * len(out_shape),
        compiler_params=SMALL,
        name="adam",
    )(*(in_vmem(v) for v in operands))


def join_kernel(*refs):
    *parts, out, sems = refs
    rows = parts[0].shape[0]
    mine = lax.axis_index("local")
    copies = []
    for i, row in enumerate((mine, 1 - mine)):
        start = 0
        for part in parts[i * len(parts) // 2 : (i + 1) * len(parts) // 2]:
            columns = pl.ds(start, part.shape[1])
            copies.append(
                pltpu.make_async_copy(
                    part, out.at[pl.ds(row * rows, rows), columns], sems.at[len(copies)]
                )
            )
            start += part.shape[1]
    for copy in copies:
        copy.start()
    for copy in copies:
        copy.wait()


def joined(grid, own):
    rows = own[0].shape[0]
    if grid.local != 2 or rows % 128:
        return lax.all_gather(jnp.concatenate(own, 1), "local", axis=0, tiled=True)
    other = []
    for part in own:
        other.append(grid.permute(part, group=1))
    vmem = pl.BlockSpec(memory_space=pltpu.VMEM)
    operands = (*own, *other)
    return pl.pallas_call(
        join_kernel,
        out_shape=jax.ShapeDtypeStruct((2 * rows, sum(p.shape[1] for p in own)), own[0].dtype),
        in_specs=[vmem] * len(operands),
        out_specs=pl.BlockSpec(memory_space=pl.ANY),
        scratch_shapes=[pltpu.SemaphoreType.DMA((len(operands),))],
        compiler_params=SMALL,
        name="join",
    )(*(in_vmem(v) for v in operands))


def step(activations, out_grads, *state):
    grid = Layout(lax.axis_size("node"), lax.axis_size("local"))
    rows = state[0].shape[0]
    count = grid.outer * grid.middle * grid.core * grid.local
    groups = grid.peers()
    odd, even = tuple(range(3, grid.outer, 2)), tuple(range(2, grid.outer, 2))
    near = tuple(range(1, min(2, grid.outer)))

    def send(messages):
        out = []
        for g, message in zip(groups, messages):
            out.append(grid.permute(message, group=g))
        return out

    rights = [out_grads] + send([out_grads] * len(groups))
    plan = {"a": odd, "b": even + near, "c": (0,)}
    plan = {name: steps for name, steps in plan.items() if steps}
    peers = (*groups, 0)
    taken = take(grid, [(g, steps) for steps in plan.values() for g in peers], rows, activations)
    lefts = {}
    for j, name in enumerate(plan):
        *messages, own = taken[j * len(peers) : (j + 1) * len(peers)]
        lefts[name] = [own] + send(messages)

    half, full = jnp.bfloat16, jnp.float32

    def sums(message, skip=0, steps=None):
        stride = len(plan[message]) * rows
        size = stride if steps is None else len(steps) * rows
        operands = rights, lefts[message]
        got = []
        if grid.core > 1:
            firsts = tuple(c * stride + skip * rows for c in range(1, grid.core))
            sent = group_sums(firsts, size, half, *operands)
            got = [grid.permute(sent[c], core=c + 1) for c in range(grid.core - 1)]
        kept = group_sums((skip * rows,), size, full, *operands)[0]
        return [kept, *got]

    def hop(parts, outer):
        part = sum([p.astype(full) for p in parts[1:]], parts[0])
        return grid.permute(part.astype(half), outer=outer)

    cols = out_grads.shape[1]
    most = cols - max(cols // CUT, 1)
    cuts = ((0, most), (most, cols - most))
    common, parts = [], [[], []]
    if odd:
        passed = hop(sums("a"), 1)
    if near:
        common.append(hop(sums("b", len(even), near), 1))
    if odd:
        total = [*sums("b", 0, even), passed]
        for j, (start, width) in enumerate(cuts):
            for i, o in enumerate(even):
                part = [p[i * rows : (i + 1) * rows, start : start + width] for p in total]
                parts[j].append(hop(part, o))
    common = sums("c") + common

    weights = []
    for j in range(2):
        weights += update(count, cuts[j : j + 1], True, state, common, parts[j : j + 1])
    new_first, new_second = update(count, cuts, False, state, common, parts)
    new_weight = joined(grid, weights)
    return (new_weight, new_first, new_second)


def solution(mesh):
    spec = P(("node", "local"), None)
    return jax.shard_map(
        step,
        mesh=mesh,
        in_specs=(spec,) * 5,
        out_specs=(P("node", None), spec, spec),
        check_vma=False,
    )
```

```python
import functools

import jax
import jax.numpy as jnp
from jax import lax
from jax.experimental import pallas as pl
from jax.experimental.pallas import tpu as pltpu
from jax.sharding import PartitionSpec as P


BLOCK = 256
LANES = 128
CUT = 4
SMALL = pltpu.CompilerParams(vmem_limit_bytes=16 * 2**20)


def quantize(values):
    blocks = values.reshape(values.shape[:-1] + (values.shape[-1] // BLOCK, BLOCK))
    largest = jnp.max(jnp.abs(blocks), axis=-1)
    scale = (largest + 1e-06) / 127.0
    payload = (blocks / scale[..., None]).astype(jnp.bfloat16)
    return (payload.reshape(values.shape), scale)


def restore_sum(payload, scale, axis):
    blocks = payload.reshape(payload.shape[:-1] + (scale.shape[-1], BLOCK))
    values = blocks.astype(jnp.float32) * scale[..., None]
    values = values.reshape(payload.shape)
    return jnp.sum(values, axis=axis)


def plain(activations, out_grads, master, first_moment, second_moment):
    node_count = lax.axis_size("node")
    local_count = lax.axis_size("local")
    own_rows = master.shape[0]
    col_count = master.shape[1]
    token_count = activations.shape[0]
    bands = activations.reshape(token_count, node_count, local_count, own_rows)
    got_inputs = lax.all_to_all(bands, "local", split_axis=2, concat_axis=0, tiled=True)
    got_outputs = lax.all_gather(out_grads, "local", axis=0, tiled=True)
    got_inputs = got_inputs.reshape(local_count, token_count, node_count * own_rows)
    got_outputs = got_outputs.reshape(local_count, token_count, col_count)
    grads = jnp.einsum("ltr,ltk->lrk", got_inputs, got_outputs, preferred_element_type=jnp.float32)
    payload, scale = quantize(grads)
    first_sum = restore_sum(payload, scale, 0).reshape(node_count, own_rows, col_count)
    second_payload, second_scale = quantize(first_sum)
    node_payload, node_scale = (
        lax.all_to_all(second_payload, "node", split_axis=0, concat_axis=0, tiled=True),
        lax.all_to_all(
            second_scale.astype(jnp.bfloat16), "node", split_axis=0, concat_axis=0, tiled=True
        ).astype(second_scale.dtype),
    )
    total = restore_sum(node_payload, node_scale, 0)
    grad_mean = total / (node_count * local_count)
    new_first = 0.9 * first_moment + 0.1 * grad_mean
    new_second = 0.95 * second_moment + 0.05 * grad_mean * grad_mean
    update = new_first / (1.0 - 0.9**10) / (jnp.sqrt(new_second / (1.0 - 0.95**10)) + 1e-08)
    own_weight = (master - 0.01 * update).astype(jnp.bfloat16)
    new_weight = lax.all_gather(own_weight, "local", axis=0, tiled=True)
    return (new_weight, new_first, new_second)


class Grid:
    def __init__(self, node_count):
        self.outer = node_count // 4
        self.count = 2 * node_count

    @staticmethod
    def fits(node_count, local_count, rows):
        outer = node_count // 4
        return (
            node_count % 4 == 0 and outer >= 4 and outer & (outer - 1) == 0 and local_count == 2
        ) and rows % LANES == 0

    def move(self, device, outer=0, core=0, first=0, second=0):
        mine = (device // 2) % 2
        local = (1 - mine) * first + mine * second
        middle = mine * first + (1 - mine) * second
        return device ^ (outer * 8 + middle * 4 + core * 2 + local)

    def permute(self, value, **flips):
        pairs = [(d, self.move(d, **flips)) for d in range(self.count)]
        return lax.ppermute(value, ("node", "local"), pairs)

    def me(self):
        return lax.axis_index("node") * 2 + lax.axis_index("local")


def in_vmem(value):
    return pltpu.with_memory_space_constraint(value, pltpu.VMEM)


def load_kernel(source, out, sem):
    copy = pltpu.make_async_copy(source, out, sem)
    copy.start()
    copy.wait()


def load(value):
    return pl.pallas_call(
        load_kernel,
        out_shape=pltpu.VMEM(value.shape, value.dtype),
        in_specs=[pl.BlockSpec(memory_space=pltpu.HBM)],
        out_specs=pl.BlockSpec(memory_space=pltpu.VMEM),
        scratch_shapes=[pltpu.SemaphoreType.DMA(())],
        compiler_params=SMALL,
        name="load",
    )(pltpu.with_memory_space_constraint(value, pltpu.HBM))


def take_kernel(grid, wanted, rows, own, partner, *outs):
    me = grid.me()
    tokens = own.shape[0]
    for (first, steps), out in zip(wanted, outs):
        at = 0
        for second, step in ((second, step) for second in range(2) for step in steps):
            block = grid.move(me, outer=step, first=first, second=second)
            columns = pl.ds(pl.multiple_of(block * rows, rows), rows)
            out[pl.ds(0, tokens), pl.ds(at, rows)] = own[:, columns]
            out[pl.ds(tokens, tokens), pl.ds(at, rows)] = partner[:, columns]
            at += rows


def take(grid, wanted, rows, own, partner):
    vmem = pl.BlockSpec(memory_space=pltpu.VMEM)
    return pl.pallas_call(
        functools.partial(take_kernel, grid, wanted, rows),
        out_shape=[
            pltpu.VMEM((2 * own.shape[0], 2 * len(steps) * rows), own.dtype) for _, steps in wanted
        ],
        in_specs=[vmem] * 2,
        out_specs=[vmem] * len(wanted),
        compiler_params=SMALL,
        name="take",
    )(in_vmem(own), in_vmem(partner))


def product(left, right):
    return lax.dot_general(
        left, right, (((0,), (0,)), ((), ())), preferred_element_type=jnp.float32
    )


def sums_kernel(first, *refs):
    lefts, rights, out = refs[:2], refs[2:-1], refs[-1]
    columns = pl.ds(first, out.shape[0])
    tokens = rights[0].shape[0]
    total = None
    for i, right in enumerate(rights):
        part = product(lefts[i // 2][pl.ds(i % 2 * tokens, tokens), columns], right[...])
        total = part if total is None else total + part
    out[...] = total.astype(out.dtype)


def sums(first, size, dtype, lefts, rights):
    vmem = pl.BlockSpec(memory_space=pltpu.VMEM)
    operands = (*lefts, *rights)
    return pl.pallas_call(
        functools.partial(sums_kernel, first),
        out_shape=pltpu.VMEM((size, rights[0].shape[1]), dtype),
        in_specs=[vmem] * len(operands),
        out_specs=vmem,
        compiler_params=SMALL,
        name="sums",
    )(*(in_vmem(v) for v in operands))


def merge_kernel(pieces, kept, got, *outs):
    for (start, size, dtype), out in zip(pieces, outs):
        at = pl.ds(start, size)
        out[...] = (kept[at, :] + got[at, :].astype(jnp.float32)).astype(dtype)


def merge(kept, got, pieces):
    vmem = pl.BlockSpec(memory_space=pltpu.VMEM)
    return pl.pallas_call(
        functools.partial(merge_kernel, pieces),
        out_shape=[pltpu.VMEM((size, kept.shape[1]), dtype) for _, size, dtype in pieces],
        in_specs=[vmem] * 2,
        out_specs=[vmem] * len(pieces),
        compiler_params=SMALL,
        name="merge",
    )(in_vmem(kept), in_vmem(got))


def adam(grad, master, first_moment, second_moment):
    new_first = 0.9 * first_moment + 0.1 * grad
    new_second = 0.95 * second_moment + 0.05 * grad * grad
    update = new_first / (1.0 - 0.9**10) / (jnp.sqrt(new_second / (1.0 - 0.95**10)) + 1e-08)
    return (master - 0.01 * update).astype(jnp.bfloat16), new_first, new_second


def update_kernel(count, cuts, weights, shared, *refs):
    master, first_moment, second_moment = refs[:3]
    common, refs = refs[3 : 3 + shared], refs[3 + shared :]
    outs = refs[-1:] if weights else refs[-2:]
    own = (len(refs) - len(outs)) // len(cuts)
    for i, (start, width) in enumerate(cuts):
        at = pl.ds(start, width)
        total = common[0][:, at]
        for part in common[1:]:
            total += part[:, at].astype(jnp.float32)
        for part in refs[i * own : (i + 1) * own]:
            total += part[...].astype(jnp.float32)
        step = adam(total / count, master[:, at], first_moment[:, at], second_moment[:, at])
        if weights:
            outs[0][...] = step[0]
        else:
            outs[0][:, at] = step[1]
            outs[1][:, at] = step[2]


def update(count, cuts, weights, state, common, parts):
    rows, cols = state[0].shape
    vmem = pl.BlockSpec(memory_space=pltpu.VMEM)
    operands = [*state, *common, *(v for part in parts for v in part)]
    if weights:
        out_shape = [pltpu.VMEM((rows, cuts[0][1]), jnp.bfloat16)]
    else:
        out_shape = [pltpu.VMEM((rows, cols), jnp.float32)] * 2
    return pl.pallas_call(
        functools.partial(update_kernel, count, cuts, weights, len(common)),
        out_shape=out_shape,
        in_specs=[vmem] * len(operands),
        out_specs=[vmem] * len(out_shape),
        compiler_params=SMALL,
        name="adam",
    )(*(in_vmem(v) for v in operands))


def join_kernel(*refs):
    *parts, out, sems = refs
    rows = parts[0].shape[0]
    mine = lax.axis_index("local")
    copies = []
    for i, row in enumerate((mine, 1 - mine)):
        start = 0
        for part in parts[i * len(parts) // 2 : (i + 1) * len(parts) // 2]:
            columns = pl.ds(start, part.shape[1])
            copies.append(
                pltpu.make_async_copy(
                    part, out.at[pl.ds(row * rows, rows), columns], sems.at[len(copies)]
                )
            )
            start += part.shape[1]
    for copy in copies:
        copy.start()
    for copy in copies:
        copy.wait()


def joined(own):
    rows = own[0].shape[0]
    pairs = [(0, 1), (1, 0)]
    other = []
    for part in own:
        other.append(lax.ppermute(part, "local", pairs))
    vmem = pl.BlockSpec(memory_space=pltpu.VMEM)
    operands = (*own, *other)
    return pl.pallas_call(
        join_kernel,
        out_shape=jax.ShapeDtypeStruct((2 * rows, sum(p.shape[1] for p in own)), own[0].dtype),
        in_specs=[vmem] * len(operands),
        out_specs=pl.BlockSpec(memory_space=pl.ANY),
        scratch_shapes=[pltpu.SemaphoreType.DMA((len(operands),))],
        compiler_params=SMALL,
        name="join",
    )(*(in_vmem(v) for v in operands))


def per_device(activations, out_grads, *state):
    node_count, local_count = lax.axis_size("node"), lax.axis_size("local")
    if not Grid.fits(node_count, local_count, state[0].shape[0]):
        return plain(activations, out_grads, *state)
    return step(Grid(node_count), activations, out_grads, *state)


def step(grid, activations, out_grads, *state):
    rows = state[0].shape[0]
    cols = out_grads.shape[1]
    odd, even = tuple(range(3, grid.outer, 2)), tuple(range(2, grid.outer, 2))
    half, full = jnp.bfloat16, jnp.float32

    partner_grads = grid.permute(out_grads, core=1)
    partner = grid.permute(activations, core=1)
    rights = [out_grads, partner_grads]
    rights += [grid.permute(v, first=1) for v in rights]
    plan = {"a": odd, "b": (*even, 1), "c": (0,)}
    own_inputs = load(activations)
    wanted = [(first, steps) for steps in plan.values() for first in range(2)]
    taken = take(grid, wanted, rows, own_inputs, partner)
    lefts = {}
    for i, name in enumerate(plan):
        own, message = taken[2 * i : 2 * i + 2]
        lefts[name] = own, grid.permute(message, first=1)

    def added(name):
        size = rows * len(plan[name])
        operands = lefts[name], rights
        sent = sums(size, size, half, *operands)
        got = grid.permute(sent, second=1)
        kept = sums(0, size, full, *operands)
        return kept, got

    def hop(parts, outer):
        part = sum([p.astype(full) for p in parts[1:]], parts[0])
        return grid.permute(part.astype(half), outer=outer)

    most = cols - cols // CUT
    cuts = ((0, most), (most, cols - most))
    split = len(even) * rows
    passed = hop(added("a"), 1)
    part, total = merge(*added("b"), ((split, rows, half), (0, split, full)))
    near = grid.permute(part, outer=1)
    parts = [
        [
            hop([p[i * rows : (i + 1) * rows, start : start + width] for p in (total, passed)], o)
            for i, o in enumerate(even)
        ]
        for start, width in cuts
    ]
    common = [*added("c"), near]

    weights = []
    for j in range(2):
        weights += update(grid.count, cuts[j : j + 1], True, state, common, parts[j : j + 1])
    new_first, new_second = update(grid.count, cuts, False, state, common, parts)
    new_weight = joined(weights)
    return (new_weight, new_first, new_second)


def solution(mesh):
    spec = P(("node", "local"), None)
    return jax.shard_map(
        per_device,
        mesh=mesh,
        in_specs=(spec,) * 5,
        out_specs=(P("node", None), spec, spec),
        check_vma=False,
    )
```

```python
import functools

import jax
import jax.numpy as jnp
from jax import lax
from jax.experimental import pallas as pl
from jax.experimental.pallas import tpu as pltpu
from jax.sharding import PartitionSpec as P


BLOCK = 256
LANES = 128
CUT = 4
SMALL = pltpu.CompilerParams(vmem_limit_bytes=16 * 2**20)


def quantize(values):
    blocks = values.reshape(values.shape[:-1] + (values.shape[-1] // BLOCK, BLOCK))
    largest = jnp.max(jnp.abs(blocks), axis=-1)
    scale = (largest + 1e-06) / 127.0
    payload = (blocks / scale[..., None]).astype(jnp.bfloat16)
    return (payload.reshape(values.shape), scale)


def restore_sum(payload, scale, axis):
    blocks = payload.reshape(payload.shape[:-1] + (scale.shape[-1], BLOCK))
    values = blocks.astype(jnp.float32) * scale[..., None]
    values = values.reshape(payload.shape)
    return jnp.sum(values, axis=axis)


def plain(activations, out_grads, master, first_moment, second_moment):
    node_count = lax.axis_size("node")
    local_count = lax.axis_size("local")
    own_rows = master.shape[0]
    col_count = master.shape[1]
    token_count = activations.shape[0]
    bands = activations.reshape(token_count, node_count, local_count, own_rows)
    got_inputs = lax.all_to_all(bands, "local", split_axis=2, concat_axis=0, tiled=True)
    got_outputs = lax.all_gather(out_grads, "local", axis=0, tiled=True)
    got_inputs = got_inputs.reshape(local_count, token_count, node_count * own_rows)
    got_outputs = got_outputs.reshape(local_count, token_count, col_count)
    grads = jnp.einsum("ltr,ltk->lrk", got_inputs, got_outputs, preferred_element_type=jnp.float32)
    payload, scale = quantize(grads)
    first_sum = restore_sum(payload, scale, 0).reshape(node_count, own_rows, col_count)
    second_payload, second_scale = quantize(first_sum)
    node_payload, node_scale = (
        lax.all_to_all(second_payload, "node", split_axis=0, concat_axis=0, tiled=True),
        lax.all_to_all(
            second_scale.astype(jnp.bfloat16), "node", split_axis=0, concat_axis=0, tiled=True
        ).astype(second_scale.dtype),
    )
    total = restore_sum(node_payload, node_scale, 0)
    grad_mean = total / (node_count * local_count)
    new_first = 0.9 * first_moment + 0.1 * grad_mean
    new_second = 0.95 * second_moment + 0.05 * grad_mean * grad_mean
    update = new_first / (1.0 - 0.9**10) / (jnp.sqrt(new_second / (1.0 - 0.95**10)) + 1e-08)
    own_weight = (master - 0.01 * update).astype(jnp.bfloat16)
    new_weight = lax.all_gather(own_weight, "local", axis=0, tiled=True)
    return (new_weight, new_first, new_second)


class Grid:
    def __init__(self, node_count):
        self.outer = node_count // 4
        self.count = 2 * node_count

    @staticmethod
    def fits(node_count, local_count, rows):
        outer = node_count // 4
        return (
            node_count % 4 == 0 and outer >= 4 and outer & (outer - 1) == 0 and local_count == 2
        ) and rows % LANES == 0

    def move(self, device, outer=0, core=0, first=0, second=0):
        mine = (device // 2) % 2
        local = (1 - mine) * first + mine * second
        middle = mine * first + (1 - mine) * second
        return device ^ (outer * 8 + middle * 4 + core * 2 + local)

    def permute(self, value, **flips):
        pairs = [(d, self.move(d, **flips)) for d in range(self.count)]
        return lax.ppermute(value, ("node", "local"), pairs)

    def me(self):
        return lax.axis_index("node") * 2 + lax.axis_index("local")


def in_vmem(value):
    return pltpu.with_memory_space_constraint(value, pltpu.VMEM)


def load_kernel(source, out, sem):
    copy = pltpu.make_async_copy(source, out, sem)
    copy.start()
    copy.wait()


def load(value):
    return pl.pallas_call(
        load_kernel,
        out_shape=pltpu.VMEM(value.shape, value.dtype),
        in_specs=[pl.BlockSpec(memory_space=pltpu.HBM)],
        out_specs=pl.BlockSpec(memory_space=pltpu.VMEM),
        scratch_shapes=[pltpu.SemaphoreType.DMA(())],
        compiler_params=SMALL,
        name="load",
    )(pltpu.with_memory_space_constraint(value, pltpu.HBM))


def take_kernel(grid, wanted, rows, own, partner, *outs):
    me = grid.me()
    tokens = own.shape[0]
    for (first, steps), out in zip(wanted, outs):
        at = 0
        for second, step in ((second, step) for second in range(2) for step in steps):
            block = grid.move(me, outer=step, first=first, second=second)
            columns = pl.ds(pl.multiple_of(block * rows, rows), rows)
            out[pl.ds(0, tokens), pl.ds(at, rows)] = own[:, columns]
            out[pl.ds(tokens, tokens), pl.ds(at, rows)] = partner[:, columns]
            at += rows


def take(grid, wanted, rows, own, partner):
    vmem = pl.BlockSpec(memory_space=pltpu.VMEM)
    return pl.pallas_call(
        functools.partial(take_kernel, grid, wanted, rows),
        out_shape=[
            pltpu.VMEM((2 * own.shape[0], 2 * len(steps) * rows), own.dtype) for _, steps in wanted
        ],
        in_specs=[vmem] * 2,
        out_specs=[vmem] * len(wanted),
        compiler_params=SMALL,
        name="take",
    )(in_vmem(own), in_vmem(partner))


def product(left, right):
    return lax.dot_general(
        left, right, (((0,), (0,)), ((), ())), preferred_element_type=jnp.float32
    )


def sums_kernel(first, *refs):
    lefts, rights, out = refs[:2], refs[2:-1], refs[-1]
    columns = pl.ds(first, out.shape[0])
    tokens = rights[0].shape[0]
    total = None
    for i, right in enumerate(rights):
        part = product(lefts[i // 2][pl.ds(i % 2 * tokens, tokens), columns], right[...])
        total = part if total is None else total + part
    out[...] = total.astype(out.dtype)


def sums(first, size, dtype, lefts, rights):
    vmem = pl.BlockSpec(memory_space=pltpu.VMEM)
    operands = (*lefts, *rights)
    return pl.pallas_call(
        functools.partial(sums_kernel, first),
        out_shape=pltpu.VMEM((size, rights[0].shape[1]), dtype),
        in_specs=[vmem] * len(operands),
        out_specs=vmem,
        compiler_params=SMALL,
        name="sums",
    )(*(in_vmem(v) for v in operands))


def merge_kernel(pieces, kept, got, *outs):
    for (start, size, dtype), out in zip(pieces, outs):
        at = pl.ds(start, size)
        out[...] = (kept[at, :] + got[at, :].astype(jnp.float32)).astype(dtype)


def merge(kept, got, pieces):
    vmem = pl.BlockSpec(memory_space=pltpu.VMEM)
    return pl.pallas_call(
        functools.partial(merge_kernel, pieces),
        out_shape=[pltpu.VMEM((size, kept.shape[1]), dtype) for _, size, dtype in pieces],
        in_specs=[vmem] * 2,
        out_specs=[vmem] * len(pieces),
        compiler_params=SMALL,
        name="merge",
    )(in_vmem(kept), in_vmem(got))


def adam(grad, master, first_moment, second_moment):
    new_first = 0.9 * first_moment + 0.1 * grad
    new_second = 0.95 * second_moment + 0.05 * grad * grad
    update = new_first / (1.0 - 0.9**10) / (jnp.sqrt(new_second / (1.0 - 0.95**10)) + 1e-08)
    return (master - 0.01 * update).astype(jnp.bfloat16), new_first, new_second


def update_kernel(count, cuts, weights, shared, *refs):
    master, first_moment, second_moment = refs[:3]
    common, refs = refs[3 : 3 + shared], refs[3 + shared :]
    outs = refs[-1:] if weights else refs[-2:]
    own = (len(refs) - len(outs)) // len(cuts)
    for i, (start, width) in enumerate(cuts):
        at = pl.ds(start, width)
        total = common[0][:, at]
        for part in common[1:]:
            total += part[:, at].astype(jnp.float32)
        for part in refs[i * own : (i + 1) * own]:
            total += part[...].astype(jnp.float32)
        step = adam(total / count, master[:, at], first_moment[:, at], second_moment[:, at])
        if weights:
            outs[0][...] = step[0]
        else:
            outs[0][:, at] = step[1]
            outs[1][:, at] = step[2]


def update(count, cuts, weights, state, common, parts):
    rows, cols = state[0].shape
    vmem = pl.BlockSpec(memory_space=pltpu.VMEM)
    operands = [*state, *common, *(v for part in parts for v in part)]
    if weights:
        out_shape = [pltpu.VMEM((rows, cuts[0][1]), jnp.bfloat16)]
    else:
        out_shape = [jax.ShapeDtypeStruct((rows, cols), jnp.float32)] * 2
    return pl.pallas_call(
        functools.partial(update_kernel, count, cuts, weights, len(common)),
        out_shape=out_shape,
        in_specs=[vmem] * len(operands),
        out_specs=[vmem] * len(out_shape),
        compiler_params=SMALL,
        name="adam",
    )(*(in_vmem(v) for v in operands))


def place_kernel(places, *refs):
    parts, out, sems = refs[: len(places)], refs[-2], refs[-1]
    mine = lax.axis_index("local")
    copies = []
    for i, (part, (other, start)) in enumerate(zip(parts, places)):
        rows, width = part.shape
        row = (1 - mine if other else mine) * rows
        copies.append(
            pltpu.make_async_copy(
                part, out.at[pl.ds(row, rows), pl.ds(start, width)], sems.at[i]
            )
        )
    for copy in copies:
        copy.start()
    for copy in copies:
        copy.wait()


def place(parts, places, shape, *held):
    return pl.pallas_call(
        functools.partial(place_kernel, places),
        out_shape=jax.ShapeDtypeStruct(shape, parts[0].dtype),
        in_specs=[pl.BlockSpec(memory_space=pltpu.VMEM)] * len(parts)
        + [pl.BlockSpec(memory_space=pl.ANY)] * len(held),
        out_specs=pl.BlockSpec(memory_space=pl.ANY),
        scratch_shapes=[pltpu.SemaphoreType.DMA((len(parts),))],
        input_output_aliases={len(parts): 0} if held else {},
        compiler_params=SMALL,
        name="join",
    )(*(in_vmem(v) for v in parts), *held)


def joined(own):
    rows, most = own[0].shape
    other = []
    for part in own:
        other.append(lax.ppermute(part, "local", [(0, 1), (1, 0)]))
    shape = (2 * rows, most + own[1].shape[1])
    held = place((*own, other[0]), ((False, 0), (False, most), (True, 0)), shape)
    return place((other[1],), ((True, most),), shape, held)


def per_device(activations, out_grads, *state):
    node_count, local_count = lax.axis_size("node"), lax.axis_size("local")
    if not Grid.fits(node_count, local_count, state[0].shape[0]):
        return plain(activations, out_grads, *state)
    return step(Grid(node_count), activations, out_grads, *state)


def step(grid, activations, out_grads, *state):
    rows = state[0].shape[0]
    cols = out_grads.shape[1]
    odd, even = tuple(range(3, grid.outer, 2)), tuple(range(2, grid.outer, 2))
    half, full = jnp.bfloat16, jnp.float32

    partner_grads = grid.permute(out_grads, core=1)
    partner = grid.permute(activations, core=1)
    rights = [out_grads, partner_grads]
    rights += [grid.permute(v, first=1) for v in rights]
    plan = {"a": odd, "b": (*even, 1), "c": (0,)}
    own_inputs = load(activations)
    wanted = [(first, steps) for steps in plan.values() for first in range(2)]
    taken = take(grid, wanted, rows, own_inputs, partner)
    lefts = {}
    for i, name in enumerate(plan):
        own, message = taken[2 * i : 2 * i + 2]
        lefts[name] = own, grid.permute(message, first=1)

    def added(name):
        size = rows * len(plan[name])
        operands = lefts[name], rights
        sent = sums(size, size, half, *operands)
        got = grid.permute(sent, second=1)
        kept = sums(0, size, full, *operands)
        return kept, got

    def hop(parts, outer):
        part = sum([p.astype(full) for p in parts[1:]], parts[0])
        return grid.permute(part.astype(half), outer=outer)

    most = cols - cols // CUT
    cuts = ((0, most), (most, cols - most))
    split = len(even) * rows
    passed = hop(added("a"), 1)
    part, total = merge(*added("b"), ((split, rows, half), (0, split, full)))
    near = grid.permute(part, outer=1)
    parts = [
        [
            hop([p[i * rows : (i + 1) * rows, start : start + width] for p in (total, passed)], o)
            for i, o in enumerate(even)
        ]
        for start, width in cuts
    ]
    common = [*added("c"), near]

    weights = []
    for j in range(2):
        weights += update(grid.count, cuts[j : j + 1], True, state, common, parts[j : j + 1])
    new_first, new_second = update(grid.count, cuts, False, state, common, parts)
    new_weight = joined(weights)
    return (new_weight, new_first, new_second)


def solution(mesh):
    spec = P(("node", "local"), None)
    return jax.shard_map(
        per_device,
        mesh=mesh,
        in_specs=(spec,) * 5,
        out_specs=(P("node", None), spec, spec),
        check_vma=False,
    )
```
